32 devices in a mesh: shard: 2 (over y), ctx: 4 (over x, core), tp: 4 (over z).
Axes of the slice: x: 2, y: 2, z: 4, core: 2. Of those that a mesh axis runs over, the one named last changes fastest.
Arguments:
- tokens_in: bfloat16 [8192, 2048], P(('shard', 'ctx'), 'tp'), may hold values from -6 to 6
- block_order: int32 [2, 8], P('shard'), may hold values from 0 to 7, as said below
- w_query: bfloat16 [2048, 2048], P(('shard', 'ctx'), 'tp'), may hold values from -0.125 to 0.125
- w_key: bfloat16 [2048, 2048], P(('shard', 'ctx'), 'tp'), may hold values from -0.125 to 0.125
- w_value: bfloat16 [2048, 2048], P(('shard', 'ctx'), 'tp'), may hold values from -0.125 to 0.125
- w_out: bfloat16 [2048, 2048], P('tp', ('shard', 'ctx')), may hold values from -0.75 to 0.75
- w_gate: bfloat16 [2048, 8192], P(('shard', 'ctx'), 'tp'), may hold values from -0.125 to 0.125
- w_up: bfloat16 [2048, 8192], P(('shard', 'ctx'), 'tp'), may hold values from -0.125 to 0.125
- w_down: bfloat16 [8192, 2048], P('tp', ('shard', 'ctx')), may hold values from -0.0625 to 0.0625
- norm_attn: bfloat16 [2048], P(('shard', 'ctx')), may hold values from 0.25 to 1.75
- norm_ffn: bfloat16 [2048], P(('shard', 'ctx')), may hold values from 0.25 to 1.75
- cotangent: bfloat16 [8192, 2048], P(('shard', 'ctx'), 'tp'), may hold values from -6 to 6
Outputs:
- layer_out: float32 [8192, 2048], P(('shard', 'ctx'), 'tp')
- grad_input: float32 [8192, 2048], P(('shard', 'ctx'), 'tp')
- grad_query: float32 [2048, 2048], P(('shard', 'ctx'), 'tp')
- grad_key: float32 [2048, 2048], P(('shard', 'ctx'), 'tp')
- grad_value: float32 [2048, 2048], P(('shard', 'ctx'), 'tp')
- grad_out: float32 [2048, 2048], P('tp', ('shard', 'ctx'))
- grad_gate: float32 [2048, 8192], P(('shard', 'ctx'), 'tp')
- grad_up: float32 [2048, 8192], P(('shard', 'ctx'), 'tp')
- grad_down: float32 [8192, 2048], P('tp', ('shard', 'ctx'))
- grad_norm_attn: float32 [2048], P(('shard', 'ctx'))
- grad_norm_ffn: float32 [2048], P(('shard', 'ctx'))
The draws below stay inside these ranges and needn't reach their ends.
Inputs may be any that keep to these rules, and one draw needn't show every extreme that they name: `block_order`: each row holds every block number once; slots 2 c and 2 c + 1 hold two blocks b and 7 - b.
All inputs are finite; a program needn't handle non-finite values.
Results may differ from the reference program's by a relative error of at most 0.025.
Values may be sent and summed in bfloat16 or wider, within the bound.
No kernel may reach another device: no remote copies, remote signals or barrier semaphores. Data moves between devices by JAX's collectives and lax.ppermute only.
A program may use at most 256 MiB of HBM per device.

```python
import math
import jax
import jax.numpy as jnp
from jax import lax

D = 2048
HD = 64
FF = 8192
HEADS = 32
HALF = 512
BLOCKS = 8
LEN = 4096
SEQS = 2
TOKENS = 8192


def draw_tokens_in(key, part):
    base_key = jax.random.fold_in(key, 11)
    noise_key = jax.random.fold_in(base_key, 0)
    return jnp.clip(jax.random.normal(noise_key, (TOKENS, D), jnp.float32), -6.0, 6.0).astype(jnp.bfloat16)


def draw_block_order(key, part):
    pair_key, flip_key = jax.random.split(jax.random.fold_in(key, 7))
    pair_count = BLOCKS // 2
    seq_keys = jax.random.split(pair_key, SEQS)
    pair_ids = jax.vmap(lambda one_key: jax.random.permutation(one_key, pair_count))(seq_keys).astype(jnp.int32)
    flip_bits = jax.random.randint(flip_key, (SEQS, pair_count), 0, 2)
    mirror = (BLOCKS - 1 - pair_ids).astype(jnp.int32)
    leading = jnp.where(flip_bits == 1, mirror, pair_ids)
    trailing = jnp.where(flip_bits == 1, pair_ids, mirror)
    return jnp.stack([leading, trailing], axis=-1).reshape(SEQS, BLOCKS).astype(jnp.int32)


def steps_of(own_key, shape, shards, low, high):
    factor_of = 1.0
    for axis_at, parts in shards:
        steps = jax.random.uniform(jax.random.fold_in(jax.random.fold_in(own_key, 6), axis_at), (parts,), jnp.float32, low / len(shards), high / len(shards))
        factor_of = factor_of * jnp.repeat(jnp.exp(steps), shape[axis_at] // parts).reshape((-1,) + (1,) * (len(shape) - 1 - axis_at))
    return factor_of


def bell_draw(key, shape, width, most, shards=(), kind=jnp.bfloat16):
    result = width * jax.random.normal(key, shape, jnp.float32)
    if shards:
        result = result * steps_of(key, shape, shards, -0.22, 0.18)
    return jnp.clip(result, -most, most).astype(kind)


def setup_inputs(seed: int = 0) -> dict:
    arg_keys = jax.random.split(jax.random.key(seed), 13)
    tokens_in = draw_tokens_in(jax.random.fold_in(arg_keys[12], 71), 0)
    block_order = draw_block_order(jax.random.fold_in(arg_keys[12], 71), 0)
    w_query = bell_draw(arg_keys[2], (D, D), D ** -0.5, 0.125, ((0, 8), (1, 4)))
    w_key = bell_draw(arg_keys[3], (D, D), D ** -0.5, 0.125, ((0, 8), (1, 4)))
    w_value = bell_draw(arg_keys[4], (D, D), D ** -0.5, 0.125, ((0, 8), (1, 4)))
    w_out = bell_draw(arg_keys[5], (D, D), (D // 32) ** -0.5, 0.75, ((0, 4), (1, 8)))
    w_gate = bell_draw(arg_keys[6], (D, FF), D ** -0.5, 0.125, ((0, 8), (1, 4)))
    w_up = bell_draw(arg_keys[7], (D, FF), D ** -0.5, 0.125, ((0, 8), (1, 4)))
    w_down = bell_draw(arg_keys[8], (FF, D), FF ** -0.5, 0.0625, ((0, 4), (1, 8)))
    norm_attn = jnp.clip(1.0 + 0.15 * jax.random.normal(arg_keys[9], (D,), jnp.float32), 0.25, 1.75).astype(jnp.bfloat16)
    norm_ffn = jnp.clip(1.0 + 0.15 * jax.random.normal(arg_keys[10], (D,), jnp.float32), 0.25, 1.75).astype(jnp.bfloat16)
    cotangent = bell_draw(arg_keys[11], (TOKENS, D), 1.0, 6.0, ((0, 8), (1, 4)))
    return {"tokens_in": tokens_in, "block_order": block_order, "w_query": w_query, "w_key": w_key, "w_value": w_value, "w_out": w_out, "w_gate": w_gate, "w_up": w_up, "w_down": w_down, "norm_attn": norm_attn, "norm_ffn": norm_ffn, "cotangent": cotangent}


@jax.custom_vjp
def low(v):
    return lax.optimization_barrier(v.astype(jnp.bfloat16)).astype(jnp.float32)

@jax.custom_vjp
def low_back(v):
    return v

def low_keep(v):
    return (low(v), None)

def low_pass(kept, grad):
    return (grad,)

def back_keep(v):
    return (v, None)

def back_low(kept, grad):
    return (low(grad),)
low.defvjp(low_keep, low_pass)
low_back.defvjp(back_keep, back_low)
theta_base = 130000.0
eps_norm = 1e-05
neg_large = -1e+30

def matmul(left_side, right_side):
    return jnp.dot(left_side, right_side, precision=lax.Precision.HIGHEST, preferred_element_type=jnp.float32)

def rms_scale(values, scaling):
    return values * lax.rsqrt(lax.optimization_barrier(jnp.mean(values * values, axis=-1, keepdims=True)) + eps_norm) * scaling

def rope_tables(positions):
    half_dim = HD // 2
    frequency = jnp.exp(jnp.arange(half_dim, dtype=jnp.float32) * (-2.0 * math.log(theta_base) / HD))
    angles = positions.astype(jnp.float32)[:, None] * frequency[None, :]
    return (jnp.cos(angles), jnp.sin(angles))

def rotate(values, cos_rows, sin_rows):
    half_dim = HD // 2
    leading = values[..., :half_dim]
    trailing = values[..., half_dim:]
    cos_wide = cos_rows[:, None, :]
    sin_wide = sin_rows[:, None, :]
    return jnp.concatenate([leading * cos_wide - trailing * sin_wide, trailing * cos_wide + leading * sin_wide], axis=-1)

def seq_positions(block_order):
    offsets = jnp.arange(LEN, dtype=jnp.int32)
    slot_ids = offsets // HALF
    block_ids = jnp.take(block_order, slot_ids, axis=1)
    return block_ids * HALF + (offsets % HALF)[None, :]

def attend_sequence(bundle):
    query_rows, key_rows, value_rows, seq_pos = bundle
    block_rows = math.gcd(LEN, 512)
    query_blocks = query_rows.reshape(LEN // block_rows, block_rows, HEADS, HD)
    pos_blocks = seq_pos.reshape(LEN // block_rows, block_rows)

    def one_block(block_pair):
        query_block, query_pos = block_pair
        scores = jnp.einsum('qhd,khd->hqk', query_block, key_rows, precision=lax.Precision.HIGHEST) * (1.0 / math.sqrt(HD))
        scores = low_back(scores)
        visible = seq_pos[None, :] <= query_pos[:, None]
        scores = jnp.where(visible[None], scores, neg_large)
        row_max = lax.optimization_barrier(jnp.max(scores, axis=-1, keepdims=True))
        weights = jnp.exp(scores - row_max)
        probability = weights / lax.optimization_barrier(jnp.sum(weights, axis=-1, keepdims=True))
        return jnp.einsum('hqk,khd->qhd', low(probability), value_rows, precision=lax.Precision.HIGHEST)
    outputs = lax.map(jax.checkpoint(one_block), (query_blocks, pos_blocks))
    return outputs.reshape(LEN, HEADS, HD)

def reference(tokens_in, block_order, w_query, w_key, w_value, w_out, w_gate, w_up, w_down, norm_attn, norm_ffn, cotangent):
    positions = seq_positions(block_order)
    cos_rows, sin_rows = rope_tables(positions.reshape(TOKENS))

    def forward(inputs, query_w, key_w, value_w, out_w, gate_w, up_w, down_w, attn_gain, ffn_gain):
        normed = low(rms_scale(inputs, attn_gain))
        query = low_back(matmul(normed, query_w)).reshape(TOKENS, HEADS, HD)
        keyed = low_back(matmul(normed, key_w)).reshape(TOKENS, HEADS, HD)
        valued = low(low_back(matmul(normed, value_w))).reshape(SEQS, LEN, HEADS, HD)
        query_rot = low(rotate(query, cos_rows, sin_rows)).reshape(SEQS, LEN, HEADS, HD)
        key_rot = low(rotate(keyed, cos_rows, sin_rows)).reshape(SEQS, LEN, HEADS, HD)
        context = lax.map(attend_sequence, (query_rot, key_rot, valued, positions))
        context_low = low(low_back(context.reshape(TOKENS, D)))
        middle = inputs + low_back(matmul(context_low, out_w))
        ffn_in = low(rms_scale(middle, ffn_gain))
        gate = low_back(matmul(ffn_in, gate_w))
        upward = low_back(matmul(ffn_in, up_w))
        hidden = low(jax.nn.silu(gate) * upward)
        return middle + matmul(hidden, down_w)
    primal = (tokens_in.astype(jnp.float32), w_query.astype(jnp.float32), w_key.astype(jnp.float32), w_value.astype(jnp.float32), w_out.astype(jnp.float32), w_gate.astype(jnp.float32), w_up.astype(jnp.float32), w_down.astype(jnp.float32), norm_attn.astype(jnp.float32), norm_ffn.astype(jnp.float32))
    layer_out, pullback = jax.vjp(forward, *primal)
    grads = pullback(cotangent.astype(jnp.float32))
    return (layer_out, grads[0], grads[1], grads[2], grads[3], grads[4], grads[5], grads[6], grads[7], grads[8], grads[9])
```

```python
import functools
import math

import jax
import jax.numpy as jnp
from jax import lax
from jax.experimental import pallas as pl
from jax.experimental.pallas import tpu as pltpu
from jax.sharding import PartitionSpec as P

HD = 64
THETA = 130000.0
EPS = 1e-05
NEG = -1e30
LANES = 128
F32 = jnp.float32
BF16 = jnp.bfloat16


def dot_nn(a, b):
    return lax.dot_general(a, b, (((1,), (0,)), ((), ())), preferred_element_type=F32)


def dot_nt(a, b):
    return lax.dot_general(a, b, (((1,), (1,)), ((), ())), preferred_element_type=F32)


def dot_tn(a, b):
    return lax.dot_general(a, b, (((0,), (0,)), ((), ())), preferred_element_type=F32)


def lane_ids(shape):
    return lax.broadcasted_iota(jnp.int32, shape, len(shape) - 1)


def spec(shape, index, **kw):
    return pl.BlockSpec(shape, index, **kw)


def whole_spec(shape):
    return pl.BlockSpec(shape, lambda *_: (0,) * len(shape), pipeline_mode=pl.Buffered(1))


ANY = pl.BlockSpec(memory_space=pl.ANY)


def call(body, name, grid, scalars, ins, in_specs, outs, out_specs, scratch=(), carry=None, flops=0):
    carry = carry or {}
    kept = list(carry.items())
    n_in, n_out = len(ins), len(outs)

    def wrapped(*refs):
        head = refs[: len(scalars)]
        rest = refs[len(scalars) :]
        data = rest[:n_in]
        tail = rest[n_in + len(kept) :]
        body(*head, *data, *tail[:n_out], *tail[n_out:])

    nbytes = sum(a.size * a.dtype.itemsize for a in ins) + sum(
        math.prod(o.shape) * o.dtype.itemsize for o in outs
    )
    return pl.pallas_call(
        wrapped,
        name=name,
        grid_spec=pltpu.PrefetchScalarGridSpec(
            num_scalar_prefetch=len(scalars),
            grid=grid,
            in_specs=list(in_specs) + [ANY] * len(kept),
            out_specs=list(out_specs),
            scratch_shapes=list(scratch),
        ),
        out_shape=list(outs),
        input_output_aliases={len(scalars) + n_in + i: o for i, (o, _) in enumerate(kept)},
        compiler_params=pltpu.CompilerParams(
            dimension_semantics=("arbitrary",) * len(grid), vmem_limit_bytes=60 * 1024 * 1024
        ),
        cost_estimate=pl.CostEstimate(flops=int(flops), bytes_accessed=int(nbytes), transcendentals=0),
    )(*scalars, *ins, *[a for _, a in kept])


def sds(shape, dtype):
    return jax.ShapeDtypeStruct(shape, dtype)


def fold_order(n):
    return list(range(0, n, 1)) if n < 3 else [0] + list(range(1, n, 2)) + list(reversed(range(2, n, 2)))


class Ring:
    def __init__(self, axis):
        n = lax.axis_size(axis)
        order = fold_order(n)
        place = {z: i for i, z in enumerate(order)}
        table = [[order[(place[z] - k) % n] for k in range(n)] for z in range(n)]
        self.axis, self.n = axis, n
        self.owners = jnp.asarray(table, jnp.int32)[lax.axis_index(axis)]
        self.pairs = [(order[i], order[(i + 1) % n]) for i in range(n)]

    def step(self, value):
        return lax.ppermute(value, self.axis, self.pairs)

    def gather(self, own):
        pieces = [own]
        for _ in range(self.n - 1):
            pieces.append(self.step(pieces[-1]))
        return pieces

    def scatter(self, pieces):
        running = pieces[1]
        for s in range(1, self.n):
            got = self.step(running)
            total = got.astype(F32) + pieces[(s + 1) % self.n].astype(F32)
            running = total.astype(BF16) if s < self.n - 1 else total
        return running

    def total(self, value):
        result, moving = value, value
        for _ in range(self.n - 1):
            moving = self.step(moving)
            result = result + moving
        return result


def turn(tile, cos, sin):
    low = lane_ids(tile.shape) % HD < HD // 2
    partner = jnp.where(low, pltpu.roll(tile, LANES - HD // 2, 1), pltpu.roll(tile, HD // 2, 1))
    return tile * cos + partner * sin


def assemble_body(n, pw, zs, *refs):
    out = refs[n]
    for k in range(n):
        out[:, pl.ds(pl.multiple_of(zs[k] * pw, pw), pw)] = refs[k][...]


def assemble(owners, pieces, tile=256):
    n = len(pieces)
    rows, pw = pieces[0].shape
    return call(
        functools.partial(assemble_body, n, pw),
        "assemble",
        (rows // tile,),
        [owners],
        pieces,
        [spec((tile, pw), lambda i, *_: (i, 0))] * n,
        [sds((rows, n * pw), pieces[0].dtype)],
        [spec((tile, n * pw), lambda i, *_: (i, 0))],
    )[0]


def qkv_body(n, pw, width, zs, *refs):
    x_pieces = refs[:n]
    gain, weight, cos_ref, sin_ref, q_out, kv_out, normed_out, full_out, inv_out = refs[n:]
    for k in range(n):
        full_out[:, pl.ds(pl.multiple_of(zs[k] * pw, pw), pw)] = x_pieces[k][...]
    x = full_out[...].astype(F32)
    inv = lax.rsqrt(jnp.mean(x * x, axis=-1, keepdims=True) + EPS)
    normed = (x * inv * gain[...]).astype(BF16)
    normed_out[...] = normed
    inv_out[...] = jnp.broadcast_to(inv, inv_out.shape)
    product = dot_nn(normed, weight[...])
    cos, sin = cos_ref[...], sin_ref[...]
    scale = 1.0 / math.sqrt(HD)
    for t in range(width // LANES):
        at = slice(t * LANES, (t + 1) * LANES)
        q_out[:, at] = (turn(product[:, at], cos, sin) * scale).astype(BF16)
        k_at = slice(width + t * LANES, width + (t + 1) * LANES)
        kv_out[:, at] = turn(product[:, k_at], cos, sin).astype(BF16)
    kv_out[:, width:] = product[:, 2 * width :].astype(BF16)


def qkv_forward(owners, pieces, gain, weight, cos, sin, tile=256):
    n = len(pieces)
    rows, pw = pieces[0].shape
    d, w3 = weight.shape
    width = w3 // 3
    row = lambda i, *_: (i, 0)
    return call(
        functools.partial(qkv_body, n, pw, width),
        "qkv_forward",
        (rows // tile,),
        [owners],
        [*pieces, gain, weight, cos, sin],
        [spec((tile, pw), row)] * n
        + [whole_spec((1, d)), whole_spec((d, w3)), spec((tile, LANES), row), spec((tile, LANES), row)],
        [
            sds((rows, width), BF16),
            sds((rows, 2 * width), BF16),
            sds((rows, d), BF16),
            sds((rows, d), BF16),
            sds((rows, LANES), F32),
        ],
        [
            spec((tile, width), row),
            spec((tile, 2 * width), row),
            spec((tile, d), row),
            spec((tile, d), row),
            spec((tile, LANES), row),
        ],
        flops=2 * rows * d * w3,
    )


def flash_step(block, q_ref, k_ref, v_ref, acc, peak, q_at, k_at, diagonal, fresh):
    q = q_ref[pl.ds(q_at, block), :]
    k = k_ref[pl.ds(k_at, block), :]
    v = v_ref[pl.ds(k_at, block), :]
    first = lane_ids((block, LANES)) < HD
    for h in range(2):
        mine = first if h == 0 else ~first
        scores = dot_nt(jnp.where(mine, q, jnp.zeros_like(q)), k)
        if diagonal:
            visible = lax.broadcasted_iota(jnp.int32, scores.shape, 0) >= lane_ids(scores.shape)
            scores = jnp.where(visible, scores, NEG)
        top = jnp.max(scores, axis=1, keepdims=True)
        rows = pl.ds(q_at, block)
        if not fresh:
            before = peak[h, rows, :]
            new = jnp.maximum(before, top)
        else:
            new = jnp.broadcast_to(top, (block, LANES))
        wide = jnp.concatenate([new] * (block // LANES), axis=1)
        weights = jnp.exp(scores - wide).astype(BF16)
        extended = jnp.where(mine, v, jnp.ones_like(v))
        update = dot_nn(weights, extended)
        if not fresh:
            update = acc[h, rows, :] * jnp.exp(before - new) + update
        acc[h, rows, :] = update
        peak[h, rows, :] = new


def attend_local_body(block, sc, q_ref, k_own, v_own, k_par, v_par, acc_out, peak_out, peak):
    low = pl.multiple_of(sc[0] * block, block)
    high = pl.multiple_of(block - sc[0] * block, block)
    step = functools.partial(flash_step, block)
    step(q_ref, k_own, v_own, acc_out, peak, low, low, True, True)
    step(q_ref, k_own, v_own, acc_out, peak, high, high, True, True)
    step(q_ref, k_own, v_own, acc_out, peak, high, low, False, False)
    peer_steps(block, sc, 1, q_ref, k_par, v_par, acc_out, peak, low, high)
    first = lane_ids(peak_out.shape) < HD
    peak_out[...] = jnp.where(first, peak[0], peak[1])


def peer_places(block, sc, at, low, high):
    peer_low = pl.multiple_of(sc[at] * block, block)
    peer_high = pl.multiple_of(block - sc[at] * block, block)
    earlier = sc[at + 1]
    q_at = pl.multiple_of(jnp.where(earlier == 1, low, high), block)
    k_at = pl.multiple_of(jnp.where(earlier == 1, peer_low, peer_high), block)
    return ((high, peer_low), (q_at, k_at))


def peer_steps(block, sc, at, q_ref, k_ref, v_ref, acc, peak, low, high):
    for q_at, k_at in peer_places(block, sc, at, low, high):
        flash_step(block, q_ref, k_ref, v_ref, acc, peak, q_at, k_at, False, False)


def attend_remote_body(block, peers, sc, q_ref, *refs):
    kv = refs[: 2 * peers]
    acc_in, peak_in, ctx_out, lse_out, acc, peak = refs[2 * peers :]
    low = pl.multiple_of(sc[0] * block, block)
    high = pl.multiple_of(block - sc[0] * block, block)
    first = lane_ids(peak_in.shape) < HD
    packed = peak_in[...]
    swapped = pltpu.roll(packed, HD, 1)
    peak[0] = jnp.where(first, packed, swapped)
    peak[1] = jnp.where(first, swapped, packed)
    acc[...] = acc_in[...]
    for j in range(peers):
        peer_steps(block, sc, 3 + 2 * j, q_ref, kv[2 * j], kv[2 * j + 1], acc, peak, low, high)
    sums = jnp.where(first, pltpu.roll(acc[0], HD, 1), pltpu.roll(acc[1], HD, 1))
    ctx_out[...] = (jnp.where(first, acc[0], acc[1]) / sums).astype(BF16)
    lse = jnp.where(first, peak[0], peak[1]) + jnp.log(sums)
    lse_t = jnp.transpose(lse)
    lse_out[0, 0:1, :] = lse_t[0:1, :]
    lse_out[0, 1:2, :] = lse_t[HD : HD + 1, :]


def attend_local(sc, q, kv_own, kv_par):
    rows, width = q.shape
    pairs, block = width // LANES, rows // 2
    head = lambda h, *_: (0, h)
    value = lambda h, *_: (0, pairs + h)
    tile = (rows, LANES)
    return call(
        functools.partial(attend_local_body, block),
        "attend_local",
        (pairs,),
        [sc],
        [q, kv_own, kv_own, kv_par, kv_par],
        [spec(tile, head), spec(tile, head), spec(tile, value), spec(tile, head), spec(tile, value)],
        [sds((2 * pairs, rows, LANES), F32), sds((rows, width), F32)],
        [spec((2, rows, LANES), lambda h, *_: (h, 0, 0)), spec(tile, head)],
        [pltpu.VMEM((2, rows, LANES), F32)],
        flops=pairs * 2 * 5 * 4 * block * block * LANES,
    )


def attend_remote(sc, q, peers, acc, peak):
    rows, width = q.shape
    pairs, block = width // LANES, rows // 2
    head = lambda h, *_: (0, h)
    value = lambda h, *_: (0, pairs + h)
    tile = (rows, LANES)
    return call(
        functools.partial(attend_remote_body, block, len(peers)),
        "attend_remote",
        (pairs,),
        [sc],
        [q, *[kv for kv in peers for _ in range(2)], acc, peak],
        [spec(tile, head)]
        + [spec(tile, head), spec(tile, value)] * len(peers)
        + [spec((2, rows, LANES), lambda h, *_: (h, 0, 0)), spec(tile, head)],
        [sds((rows, width), BF16), sds((pairs, 8, rows), F32)],
        [spec(tile, head), spec((1, 8, rows), lambda h, *_: (h, 0, 0))],
        [pltpu.VMEM((2, rows, LANES), F32), pltpu.VMEM((2, rows, LANES), F32)],
        flops=pairs * 2 * 2 * len(peers) * 4 * block * block * LANES,
    )


def out_body(n, pw, rows, zs, *refs):
    ctx = refs[:n]
    weight, x_ref, gain, normed_out, mid_out, own_out, inv_out, wide = refs[n:]
    j = pl.program_id(0)
    steps = pl.num_programs(0)
    dw = weight.shape[0]
    at = pl.ds(pl.multiple_of(j * dw, dw), dw)
    hw = ctx[0].shape[1]
    total = x_ref[...].astype(F32)
    for k in range(n):
        total = total + dot_nt(ctx[k][...], weight[:, k * hw : (k + 1) * hw])
    wide[:, at] = total
    mid_out[...] = total

    @pl.when(j == steps - 1)
    def _():
        middle = wide[...]
        inv = lax.rsqrt(jnp.mean(middle * middle, axis=-1, keepdims=True) + EPS)
        normed_out[...] = (middle * inv * gain[...]).astype(BF16)
        inv_out[...] = jnp.broadcast_to(inv, inv_out.shape)
        own_out[...] = wide[:, pl.ds(pl.multiple_of(zs[0] * pw, pw), pw)]


def out_forward(owners, chunk, ctx_pieces, weight, x_full, gain, carry):
    n = len(ctx_pieces)
    rows, hw = ctx_pieces[0].shape
    total_rows, d = x_full.shape
    pw = d // n
    dw = 512
    fixed = lambda j, *_: (0, 0)
    return call(
        functools.partial(out_body, n, pw, rows),
        "out_forward",
        (d // dw,),
        [owners],
        [*ctx_pieces, weight, x_full, gain],
        [spec((rows, hw), fixed)] * n
        + [spec((dw, n * hw), lambda j, *_: (j, 0)), spec((rows, dw), lambda j, *_: (chunk, j)), whole_spec((1, d))],
        [sds((total_rows, d), BF16), sds((rows, d), F32), sds((rows, pw), F32), sds((rows, LANES), F32)],
        [
            spec((rows, d), lambda j, *_: (chunk, 0)),
            spec((rows, dw), lambda j, *_: (0, j)),
            spec((rows, pw), fixed),
            spec((rows, LANES), fixed),
        ],
        [pltpu.VMEM((rows, d), F32)],
        carry=carry,
        flops=2 * rows * d * n * hw,
    )


def gate_body(normed, w_gate, w_up, hidden_out, gate_out, up_out):
    x = normed[...]
    gate = dot_nn(x, w_gate[...])
    up = dot_nn(x, w_up[...])
    gate_out[...] = gate
    up_out[...] = up
    hidden_out[...] = (gate * jax.nn.sigmoid(gate) * up).astype(BF16)


def gate_forward(chunk, chunks, normed, w_gu, carry, tile=512):
    total_rows, d = normed.shape
    rows = total_rows // chunks
    ff = w_gu.shape[1] // 2
    steps = ff // tile
    return call(
        gate_body,
        "gate_forward",
        (steps,),
        [],
        [normed, w_gu, w_gu],
        [
            spec((rows, d), lambda j: (chunk, 0)),
            spec((d, tile), lambda j: (0, j)),
            spec((d, tile), lambda j: (0, steps + j)),
        ],
        [sds((total_rows, ff), BF16), sds((rows, ff), F32), sds((rows, ff), F32)],
        [spec((rows, tile), lambda j: (chunk, j)), spec((rows, tile), lambda j: (0, j)), spec((rows, tile), lambda j: (0, j))],
        carry=carry,
        flops=4 * rows * d * ff,
    )


def ffn_back_body(n, pw, zs, dy_ref, gate_ref, up_ref, w_down, w_gate, w_up, dgate_out, dup_out, *refs):
    pieces = refs[:n]
    acc = refs[n]
    j = pl.program_id(0)
    grad_hidden = dot_nn(dy_ref[...], w_down[...])
    gate, up = gate_ref[...], up_ref[...]
    sig = jax.nn.sigmoid(gate)
    dgate = (grad_hidden * up * sig * (1.0 + gate * (1.0 - sig))).astype(BF16)
    dup = (grad_hidden * gate * sig).astype(BF16)
    dgate_out[...] = dgate
    dup_out[...] = dup
    update = dot_nt(dgate, w_gate[...]) + dot_nt(dup, w_up[...])

    @pl.when(j == 0)
    def _():
        acc[...] = update

    @pl.when(j > 0)
    def _():
        acc[...] += update

    @pl.when(j == pl.num_programs(0) - 1)
    def _():
        for k in range(n):
            pieces[k][...] = acc[:, pl.ds(pl.multiple_of(zs[k] * pw, pw), pw)].astype(BF16)


def ffn_back(owners, n, chunk, dy, gate, up, w_down_t, w_gu, carry, tile=512):
    total_rows, d = dy.shape
    rows, ff = gate.shape
    pw = d // n
    steps = ff // tile
    fixed = lambda j, *_: (0, 0)
    return call(
        functools.partial(ffn_back_body, n, pw),
        "ffn_back",
        (steps,),
        [owners],
        [dy, gate, up, w_down_t, w_gu, w_gu],
        [
            spec((rows, d), lambda j, *_: (chunk, 0)),
            spec((rows, tile), lambda j, *_: (0, j)),
            spec((rows, tile), lambda j, *_: (0, j)),
            spec((d, tile), lambda j, *_: (0, j)),
            spec((d, tile), lambda j, *_: (0, j)),
            spec((d, tile), lambda j, *_: (0, steps + j)),
        ],
        [sds((total_rows, ff), BF16), sds((total_rows, ff), BF16)] + [sds((rows, pw), BF16)] * n,
        [spec((rows, tile), lambda j, *_: (chunk, j))] * 2 + [spec((rows, pw), fixed)] * n,
        [pltpu.VMEM((rows, d), F32)],
        carry=carry,
        flops=6 * rows * d * ff,
    )


def down_body(n, zs, hidden, w_down, *refs):
    k = pl.program_id(0)
    product = dot_nt(hidden[...], w_down[...]).astype(BF16)
    for i in range(n):

        @pl.when(k == i)
        def _(i=i):
            refs[i][...] = product


def down_forward(owners, n, hidden, w_down_t):
    rows, ff = hidden.shape
    d = w_down_t.shape[0]
    pw = d // n
    fixed = lambda k, *_: (0, 0)
    return call(
        functools.partial(down_body, n),
        "down_forward",
        (n,),
        [owners],
        [hidden, w_down_t],
        [whole_spec((rows, ff)), spec((pw, ff), lambda k, zs: (zs[k], 0))],
        [sds((rows, pw), BF16)] * n,
        [spec((rows, pw), fixed)] * n,
        flops=2 * rows * d * ff,
    )


def mid_back_body(n, pw, zs, *refs):
    g_pieces = refs[:n]
    dy_ref, mid_ref, inv_ref, gain, weight, low_out, dctx_out, own_out, gain_out, g_full = refs[n:]
    i = pl.program_id(0)
    for k in range(n):
        g_full[:, pl.ds(pl.multiple_of(zs[k] * pw, pw), pw)] = g_pieces[k][...].astype(F32)
    g = g_full[...]
    middle = mid_ref[...]
    inv = inv_ref[:, 0:1]
    u2 = g * gain[...]
    inner = jnp.sum(u2 * middle, axis=-1, keepdims=True)
    part = jnp.sum(g * middle * inv, axis=0, keepdims=True)

    @pl.when(i == 0)
    def _():
        gain_out[...] = part

    @pl.when(i > 0)
    def _():
        gain_out[...] += part

    grad_mid = dy_ref[...].astype(F32) + inv * u2 - middle * (inv * inv * inv) * (inner / middle.shape[-1])
    low = grad_mid.astype(BF16)
    low_out[...] = low
    g_full[...] = grad_mid
    own_out[...] = g_full[:, pl.ds(pl.multiple_of(zs[0] * pw, pw), pw)]
    dctx_out[...] = dot_nn(low, weight[...]).astype(BF16)


def mid_back(owners, chunk, g_pieces, dy, middle, inv, gain, w_out_rel, width, carry, tile=256):
    n = len(g_pieces)
    rows, pw = g_pieces[0].shape
    total_rows, d = dy.shape
    per = rows // tile
    row = lambda i, *_: (i, 0)
    wide_row = lambda i, *_: (chunk * per + i, 0)
    return call(
        functools.partial(mid_back_body, n, pw),
        "mid_back",
        (per,),
        [owners],
        [*g_pieces, dy, middle, inv, gain, w_out_rel],
        [spec((tile, pw), row)] * n
        + [
            spec((tile, d), wide_row),
            spec((tile, d), row),
            spec((tile, LANES), row),
            whole_spec((1, d)),
            whole_spec((d, width)),
        ],
        [sds((total_rows, d), BF16), sds((total_rows, width), BF16), sds((rows, pw), F32), sds((1, d), F32)],
        [spec((tile, d), wide_row), spec((tile, width), wide_row), spec((tile, pw), row), spec((1, d), lambda i, *_: (0, 0))],
        [pltpu.VMEM((tile, d), F32)],
        carry=carry,
        flops=2 * rows * d * width,
    )


def back_step(block, q_ref, do_ref, lse_ref, delta, k_ref, v_ref, dq, dk, dv, q_at, k_at, diagonal):
    q_rows, k_rows = pl.ds(q_at, block), pl.ds(k_at, block)
    q, do = q_ref[q_rows, :], do_ref[q_rows, :]
    k, v = k_ref[k_rows, :], v_ref[k_rows, :]
    first = lane_ids((block, LANES)) < HD
    none = jnp.zeros_like(q)
    dq_new, dk_new, dv_new = dq[q_rows, :], dk[k_rows, :], dv[k_rows, :]
    for h in range(2):
        mine = first if h == 0 else ~first
        k_h = jnp.where(mine, k, none)
        scores = dot_nt(k_h, q)
        probs = jnp.exp(scores - lse_ref[0, h : h + 1, q_rows])
        if diagonal:
            visible = lane_ids(scores.shape) >= lax.broadcasted_iota(jnp.int32, scores.shape, 0)
            probs = jnp.where(visible, probs, 0.0)
        dprobs = dot_nt(jnp.where(mine, v, none), do)
        dscores = (probs * (dprobs - delta[h : h + 1, q_rows])).astype(BF16)
        dv_new = dv_new + dot_nn(probs.astype(BF16), jnp.where(mine, do, none))
        dk_new = dk_new + dot_nn(dscores, jnp.where(mine, q, none))
        dq_new = dq_new + dot_tn(dscores, k_h)
    dq[q_rows, :] = dq_new
    dk[k_rows, :] = dk_new
    dv[k_rows, :] = dv_new


def row_delta(do_ref, ctx_ref, delta):
    product = do_ref[...].astype(F32) * ctx_ref[...].astype(F32)
    head = lax.broadcasted_iota(jnp.int32, (8, LANES), 0)
    picks = (lane_ids((8, LANES)) // HD == head).astype(F32)
    delta[...] = lax.dot_general(
        picks, product, (((1,), (1,)), ((), ())), precision=lax.Precision.HIGHEST, preferred_element_type=F32
    )


def attend_back_remote_body(block, peers, sc, q_ref, do_ref, ctx_ref, lse_ref, *refs):
    kv = refs[: 2 * peers]
    dq_out = refs[2 * peers]
    outs = refs[2 * peers + 1 : 4 * peers + 1]
    delta, acc = refs[4 * peers + 1 :]
    low = pl.multiple_of(sc[0] * block, block)
    high = pl.multiple_of(block - sc[0] * block, block)
    row_delta(do_ref, ctx_ref, delta)
    dq_out[...] = jnp.zeros_like(dq_out)
    acc[...] = jnp.zeros_like(acc)
    for j in range(peers):
        dk, dv = acc.at[2 * j], acc.at[2 * j + 1]
        for q_at, k_at in peer_places(block, sc, 3 + 2 * j, low, high):
            back_step(block, q_ref, do_ref, lse_ref, delta, kv[2 * j], kv[2 * j + 1], dq_out, dk, dv, q_at, k_at, False)
        outs[2 * j][...] = dk[...].astype(BF16)
        outs[2 * j + 1][...] = dv[...].astype(BF16)


def attend_back_remote(sc, q, do, ctx, lse, peers):
    rows, width = q.shape
    pairs, block = width // LANES, rows // 2
    head = lambda h, *_: (0, h)
    value = lambda h, *_: (0, pairs + h)
    tile = (rows, LANES)
    m = len(peers)
    return call(
        functools.partial(attend_back_remote_body, block, m),
        "attend_back_remote",
        (pairs,),
        [sc],
        [q, do, ctx, lse, *[kv for kv in peers for _ in range(2)]],
        [spec(tile, head)] * 3
        + [spec((1, 8, rows), lambda h, *_: (h, 0, 0))]
        + [spec(tile, head), spec(tile, value)] * m,
        [sds((rows, width), F32)] + [sds((rows, width), BF16)] * (2 * m),
        [spec(tile, head)] * (1 + 2 * m),
        [pltpu.VMEM((8, rows), F32), pltpu.VMEM((2 * m, rows, LANES), F32)],
        flops=pairs * 2 * 2 * m * 10 * block * block * LANES,
    )


def attend_back_local_body(block, sc, q_ref, do_ref, ctx_ref, lse_ref, k_own, v_own, k_par, v_par, dq_in, cos, sin, *refs):
    dq_out, dot_out, dk_out, dv_out, dkp_out, dvp_out, delta, dq, acc = refs
    low = pl.multiple_of(sc[0] * block, block)
    high = pl.multiple_of(block - sc[0] * block, block)
    row_delta(do_ref, ctx_ref, delta)
    dq[...] = dq_in[...]
    dk_out[...] = jnp.zeros_like(dk_out)
    dv_out[...] = jnp.zeros_like(dv_out)
    acc[...] = jnp.zeros_like(acc)
    step = functools.partial(back_step, block, q_ref, do_ref, lse_ref, delta)
    for q_at, k_at in peer_places(block, sc, 1, low, high):
        step(k_par, v_par, dq, acc.at[0], acc.at[1], q_at, k_at, False)
    dkp_out[...] = acc[0].astype(BF16)
    dvp_out[...] = acc[1].astype(BF16)
    step(k_own, v_own, dq, dk_out, dv_out, low, low, True)
    step(k_own, v_own, dq, dk_out, dv_out, high, high, True)
    step(k_own, v_own, dq, dk_out, dv_out, high, low, False)
    total = dq[...]
    part = total * q_ref[...].astype(F32)

    @pl.when(pl.program_id(0) == 0)
    def _():
        dot_out[...] = part

    @pl.when(pl.program_id(0) > 0)
    def _():
        dot_out[...] += part

    dq_out[...] = turn(total * (1.0 / math.sqrt(HD)), cos[...], -sin[...]).astype(BF16)


def attend_back_local(sc, q, do, ctx, lse, kv_own, kv_par, dq, cos, sin):
    rows, width = q.shape
    pairs, block = width // LANES, rows // 2
    head = lambda h, *_: (0, h)
    value = lambda h, *_: (0, pairs + h)
    tile = (rows, LANES)
    return call(
        functools.partial(attend_back_local_body, block),
        "attend_back_local",
        (pairs,),
        [sc],
        [q, do, ctx, lse, kv_own, kv_own, kv_par, kv_par, dq, cos, sin],
        [spec(tile, head)] * 3
        + [spec((1, 8, rows), lambda h, *_: (h, 0, 0))]
        + [spec(tile, head), spec(tile, value)] * 2
        + [spec(tile, head), whole_spec(tile), whole_spec(tile)],
        [sds((rows, width), BF16), sds((rows, LANES), F32)]
        + [sds((rows, width), F32)] * 2
        + [sds((rows, width), BF16)] * 2,
        [spec(tile, head), spec(tile, lambda h, *_: (0, 0))] + [spec(tile, head)] * 4,
        [pltpu.VMEM((8, rows), F32), pltpu.VMEM(tile, F32), pltpu.VMEM((2, rows, LANES), F32)],
        flops=pairs * 2 * 5 * 10 * block * block * LANES,
    )


def qkv_back_body(n, pw, width, extra, zs, *refs):
    dq, dots, dk, dv, kv = refs[:5]
    more = refs[5 : 5 + 2 * extra]
    cos, sin, weight = refs[5 + 2 * extra : 8 + 2 * extra]
    delta_out, sum_out = refs[8 + 2 * extra : 10 + 2 * extra]
    pieces = refs[10 + 2 * extra :]
    dk_all, dv_all = dk[...], dv[...]
    for e in range(extra):
        dk_all = dk_all + more[2 * e][...].astype(F32)
        dv_all = dv_all + more[2 * e + 1][...].astype(F32)
    part = dots[...]
    for t in range(width // LANES):
        at = slice(t * LANES, (t + 1) * LANES)
        v_at = slice(width + t * LANES, width + (t + 1) * LANES)
        part = part + dk_all[:, at] * kv[:, at].astype(F32) + dv_all[:, at] * kv[:, v_at].astype(F32)
        delta_out[:, at] = dq[:, at]
        delta_out[:, v_at] = turn(dk_all[:, at], cos[...], -sin[...]).astype(BF16)
    delta_out[:, 2 * width :] = dv_all.astype(BF16)
    sum_out[...] = jnp.broadcast_to(jnp.sum(part, axis=1, keepdims=True), sum_out.shape)
    delta = delta_out[...]
    for k in range(n):
        rows = pl.ds(pl.multiple_of(zs[k] * pw, pw), pw)
        pieces[k][...] = dot_nt(delta, weight[rows, :]).astype(BF16)


def qkv_back(owners, n, chunk, chunks, dq, dots, dk, dv, kv, more, cos, sin, weight, carry, tile=256):
    total_rows, width = dq.shape
    rows = total_rows // chunks
    d, w3 = weight.shape
    pw = d // n
    per = rows // tile
    here = lambda i, *_: (chunk * per + i, 0)
    row = lambda i, *_: (i, 0)
    extra = len(more) // 2
    return call(
        functools.partial(qkv_back_body, n, pw, width, extra),
        "qkv_back",
        (per,),
        [owners],
        [dq, dots, dk, dv, kv, *more, cos, sin, weight],
        [spec((tile, width), here), spec((tile, LANES), here), spec((tile, width), here), spec((tile, width), here)]
        + [spec((tile, 2 * width), here)]
        + [spec((tile, width), here)] * (2 * extra)
        + [spec((tile, LANES), here)] * 2
        + [whole_spec((d, w3))],
        [sds((total_rows, w3), BF16), sds((rows, LANES), F32)] + [sds((rows, pw), BF16)] * n,
        [spec((tile, w3), here), spec((tile, LANES), row)] + [spec((tile, pw), row)] * n,
        carry=carry,
        flops=2 * rows * d * w3,
    )


def wgrad(left, right):
    return jnp.einsum("ta,tb->ab", left, right, preferred_element_type=F32).astype(BF16)


def per_device(
    tokens_in, block_order, w_query, w_key, w_value, w_out, w_gate, w_up, w_down, norm_attn, norm_ffn, cotangent
):
    world = ("shard", "ctx")
    n_ctx = lax.axis_size("ctx")
    c = lax.axis_index("ctx")
    ring = Ring("tp")
    n = ring.n
    rows = tokens_in.shape[0]
    block = rows // 2
    pw = tokens_in.shape[1]
    width = w_query.shape[1]
    ff = w_gate.shape[1]
    chunks = 2

    w_out_rel = jnp.concatenate(ring.gather(jnp.transpose(w_out)), axis=1)
    x_pieces = ring.gather(tokens_in)
    w_qkv = lax.all_gather(jnp.concatenate([w_query, w_key, w_value], axis=1), world, axis=0, tiled=True)
    gains = lax.all_gather(jnp.stack([norm_attn, norm_ffn]), world, axis=1, tiled=True).astype(F32)
    w_gu = lax.all_gather(jnp.concatenate([w_gate, w_up], axis=1), world, axis=0, tiled=True)
    w_out_t = lax.all_gather(w_out_rel, world, axis=0, tiled=True)
    w_down_t = lax.all_gather(jnp.transpose(w_down), world, axis=0, tiled=True)
    attn_gain, ffn_gain = gains[0:1], gains[1:2]

    order = block_order[0]
    pair_ids = lax.dynamic_slice_in_dim(order, 2 * c, 2)
    positions = (pair_ids[:, None] * block + jnp.arange(block, dtype=jnp.int32)[None, :]).reshape(rows)
    half = HD // 2
    frequency = jnp.exp(jnp.arange(half, dtype=F32) * (-2.0 * math.log(THETA) / HD))
    angles = positions.astype(F32)[:, None] * frequency[None, :]
    cos1, sin1 = jnp.cos(angles), jnp.sin(angles)
    cos = jnp.concatenate([cos1, cos1, cos1, cos1], axis=1)
    sin = jnp.concatenate([-sin1, sin1, -sin1, sin1], axis=1)

    chips = n_ctx // 2
    partner = [(i, i ^ 1) for i in range(n_ctx)]
    shift = [[(i, (i + 2 * k) % n_ctx) for i in range(n_ctx)] for k in range(chips)]
    lows = (order[0::2] > order[1::2]).astype(jnp.int32)
    starts = jnp.minimum(order[0::2], order[1::2])
    ids = [c, c ^ 1]
    for k in range(1, chips):
        ids += [(c - 2 * k) % n_ctx, ((c ^ 1) - 2 * k) % n_ctx]
    ids = jnp.stack(ids)
    slot = lows[ids]
    earlier = (starts[ids] < starts[c]).astype(jnp.int32)
    sc = jnp.stack([slot, earlier], axis=1).reshape(-1)
    sc = jnp.concatenate([sc[0:1], sc[2:]])

    q, kv, normed_attn, x_full, inv_attn = qkv_forward(ring.owners, x_pieces, attn_gain, w_qkv, cos, sin)
    kv_par = lax.ppermute(kv, "ctx", partner)
    far = []
    for k in range(1, chips):
        got = lax.ppermute(kv, "ctx", shift[k])
        far += [got, lax.ppermute(got, "ctx", partner)]
    acc, peak = attend_local(sc, q, kv, kv_par)
    ctx, lse = attend_remote(sc, q, far, acc, peak)

    crows = rows // chunks
    ctx_pieces = [ring.gather(ctx[i * crows : (i + 1) * crows]) for i in range(chunks)]
    dy = assemble(ring.owners, ring.gather(cotangent))
    normed_ffn = hidden = None
    mids, mid_own, inv_ffn, gates, ups = [], [], [], [], []
    for i in range(chunks):
        normed_ffn, mid, own, inv = out_forward(
            ring.owners, i, ctx_pieces[i], w_out_t, x_full, ffn_gain, {} if i == 0 else {0: normed_ffn}
        )
        mids.append(mid)
        mid_own.append(own)
        inv_ffn.append(inv)
        hidden, gate, up = gate_forward(i, chunks, normed_ffn, w_gu, {} if i == 0 else {0: hidden})
        gates.append(gate)
        ups.append(up)

    dgate = dup = None
    grads_mid = []
    for i in range(chunks):
        dgate, dup, *pieces = ffn_back(
            ring.owners, n, i, dy, gates[i], ups[i], w_down_t, w_gu, {} if i == 0 else {0: dgate, 1: dup}
        )
        grads_mid.append(ring.gather(ring.scatter(pieces).astype(BF16)))

    grad_down_t = wgrad(dy, hidden)
    s_down = lax.psum_scatter(grad_down_t, world, scatter_dimension=0, tiled=True)
    grad_gu = wgrad(normed_ffn, jnp.concatenate([dgate, dup], axis=1))
    s_gu = lax.psum_scatter(grad_gu, world, scatter_dimension=0, tiled=True)
    branch = ring.scatter(down_forward(ring.owners, n, hidden, w_down_t))
    layer_out = jnp.concatenate(mid_own, axis=0) + branch

    low = dctx = None
    gm_own, gain_parts = [], []
    for i in range(chunks):
        low, dctx, own, part = mid_back(
            ring.owners, i, grads_mid[i], dy, mids[i], inv_ffn[i], ffn_gain, w_out_t, width,
            {} if i == 0 else {0: low, 1: dctx},
        )
        gm_own.append(own)
        gain_parts.append(part)
    grad_out_t = wgrad(low, ctx)
    s_out = lax.psum_scatter(grad_out_t, world, scatter_dimension=0, tiled=True)

    dq, *parts = attend_back_remote(sc, q, dctx, ctx, lse, far)
    more = []
    for k in range(1, chips):
        same, other = parts[4 * (k - 1) : 4 * k - 2], parts[4 * k - 2 : 4 * k]
        back = [(b, a) for a, b in shift[k]]
        for mine, theirs in zip(same, other):
            joined = mine.astype(F32) + lax.ppermute(theirs, "ctx", partner).astype(F32)
            more.append(lax.ppermute(joined.astype(BF16), "ctx", back))
    delta_q, dots, dk, dv, dk_par, dv_par = attend_back_local(sc, q, dctx, ctx, lse, kv, kv_par, dq, cos, sin)
    more += [lax.ppermute(dk_par, "ctx", partner), lax.ppermute(dv_par, "ctx", partner)]

    delta = None
    grad_input, attn_parts = [], []
    for i in range(chunks):
        delta, sums, *pieces = qkv_back(
            ring.owners, n, i, chunks, delta_q, dots, dk, dv, kv, more, cos, sin, w_qkv,
            {} if i == 0 else {0: delta},
        )
        inner = ring.total(sums[:, 0])[:, None]
        g = ring.scatter(pieces)
        at = slice(i * crows, (i + 1) * crows)
        x = tokens_in[at].astype(F32)
        inv = inv_attn[at, 0:1]
        own_gain = lax.dynamic_slice_in_dim(attn_gain, lax.axis_index("tp") * pw, pw, 1)
        grad_input.append(gm_own[i] + inv * (g * own_gain) - x * (inv * inv) * (inner / (n * pw)))
        attn_parts.append(jnp.sum(g * x * inv, axis=0, keepdims=True))
    grad_input = jnp.concatenate(grad_input, axis=0)

    grad_qkv = wgrad(normed_attn, delta)
    s_qkv = lax.psum_scatter(grad_qkv, world, scatter_dimension=0, tiled=True)

    own_part = sum(attn_parts)
    placed = lax.dynamic_update_slice_in_dim(jnp.zeros((1, n * pw), F32), own_part, lax.axis_index("tp") * pw, 1)
    ffn_part = jnp.where(lax.axis_index("tp") == 0, 1.0, 0.0) * sum(gain_parts)
    both = lax.psum(jnp.concatenate([placed, ffn_part], axis=0), ("shard", "ctx", "tp"))
    own = w_query.shape[0]
    first = (lax.axis_index("shard") * n_ctx + c) * own
    both = lax.dynamic_slice_in_dim(both, first, own, 1)

    s_qkv = s_qkv.astype(F32)
    s_gu = s_gu.astype(F32)
    return (
        layer_out,
        grad_input,
        s_qkv[:, :width],
        s_qkv[:, width : 2 * width],
        s_qkv[:, 2 * width :],
        jnp.transpose(s_out.astype(F32)),
        s_gu[:, :ff],
        s_gu[:, ff:],
        jnp.transpose(s_down.astype(F32)),
        both[0],
        both[1],
    )


def solution(mesh):
    rows = P(("shard", "ctx"), "tp")
    cols = P("tp", ("shard", "ctx"))
    gain = P(("shard", "ctx"))
    return jax.shard_map(
        per_device,
        mesh=mesh,
        in_specs=(rows, P("shard", None), rows, rows, rows, cols, rows, rows, cols, gain, gain, rows),
        out_specs=(rows, rows, rows, rows, rows, cols, rows, rows, cols, gain, gain),
        check_vma=False,
    )
```
